32 devices in a mesh: cuts: 2 (over x), gz: 16 (over z, y, core).
Axes of the slice: x: 2, y: 2, z: 4, core: 2. Of those that a mesh axis runs over, the one named last changes fastest.
Arguments:
- states: float32 [2, 64, 32, 256], P('cuts', 'gz'), may hold values from -8 to 8
- conduct: float32 [64, 32, 256], P('gz'), may hold values from 0.5 to 4
Outputs:
- end_states: float32 [2, 64, 32, 256], P('cuts', 'gz')
The draws below stay inside these ranges and needn't reach their ends.
All inputs are finite; a program needn't handle non-finite values.
Results may differ from the reference program's by a relative error of at most 0.0001.
Values sent between devices are 32-bit elements; how exact they have to be, the bound alone decides.
A program may use at most 64 MiB of HBM per device.

```python
import math
import jax
import jax.numpy as jnp
from jax import lax

NX = 32
NY = 256
STEPS = 2
SWEEPS = 3
SWEEPS_C = 2
SLICES = 2
NZ = 64


def draw_states(key, part):
    base = jax.random.normal(key, (SLICES, NZ, NX, NY), jnp.float32)
    return jnp.clip(base, -8.0, 8.0)


def level_of(own_key, extent, cuts, smallest, high):
    loudness = 1.0
    for axis_at, shards_of in cuts:
        draws = jax.random.uniform(jax.random.fold_in(jax.random.fold_in(own_key, 6), axis_at), (shards_of,), jnp.float32, smallest / len(cuts), high / len(cuts))
        loudness = loudness * jnp.repeat(jnp.exp(draws), extent[axis_at] // shards_of).reshape((-1,) + (1,) * (len(extent) - 1 - axis_at))
    return loudness


def setup_inputs(seed: int = 0) -> dict:
    arg_keys = jax.random.split(jax.random.key(seed), 3)
    states = draw_states(jax.random.fold_in(arg_keys[2], 71), 0)
    conduct = jnp.clip(jnp.exp(math.log(4.0) - 2.0794415 * jax.random.uniform(arg_keys[1], (NZ, NX, NY), jnp.float32) ** level_of(arg_keys[1], (NZ, NX, NY), ((0, 16),), -0.2, 0.2)), 0.5, 4.0)
    return {"states": states, "conduct": conduct}


COUPLING = 1.0
SPREAD = 0.85


def chebyshev_weights(count):
    return [1.0 / (1.0 + SPREAD * math.cos(math.pi * (2 * index_now + 1) / (2 * count))) for index_now in range(count)]


def face_terms(conduct):
    padded = jnp.pad(conduct, 1)
    center = conduct
    lower_z = 0.5 * (center + padded[:-2, 1:-1, 1:-1])
    upper_z = 0.5 * (center + padded[2:, 1:-1, 1:-1])
    lower_x = 0.5 * (center + padded[1:-1, :-2, 1:-1])
    upper_x = 0.5 * (center + padded[1:-1, 2:, 1:-1])
    lower_y = 0.5 * (center + padded[1:-1, 1:-1, :-2])
    upper_y = 0.5 * (center + padded[1:-1, 1:-1, 2:])
    return (lower_z, upper_z, lower_x, upper_x, lower_y, upper_y)


def diagonal_of(faces, coupling):
    return 1.0 + coupling * (faces[0] + faces[1] + faces[2] + faces[3] + faces[4] + faces[5])


def operate(iterate, faces, diagonal, coupling):
    padded = jnp.pad(iterate, 1)
    beside_all = (faces[0] * padded[:-2, 1:-1, 1:-1] + faces[1] * padded[2:, 1:-1, 1:-1]
              + faces[2] * padded[1:-1, :-2, 1:-1] + faces[3] * padded[1:-1, 2:, 1:-1]
              + faces[4] * padded[1:-1, 1:-1, :-2] + faces[5] * padded[1:-1, 1:-1, 2:])
    return diagonal * iterate - coupling * beside_all


def implicit_solve(source, faces, diagonal, coupling, weights):
    iterate = source
    for weight in weights:
        iterate = iterate + weight * (source - operate(iterate, faces, diagonal, coupling)) / diagonal
    return iterate


def restrict(field):
    shaped = field.reshape(field.shape[0] // 2, 2, field.shape[1] // 2, 2, field.shape[2] // 2, 2)
    return shaped.mean(axis=(1, 3, 5))


def prolong(coarse):
    return jnp.repeat(jnp.repeat(jnp.repeat(coarse, 2, axis=0), 2, axis=1), 2, axis=2)


def reference(states, conduct):
    fine_faces = face_terms(conduct)
    fine_diag = diagonal_of(fine_faces, COUPLING)
    coarse_faces = face_terms(restrict(conduct))
    coarse_diag = diagonal_of(coarse_faces, 0.5 * COUPLING)
    fine_weights = chebyshev_weights(SWEEPS)
    coarse_weights = chebyshev_weights(SWEEPS_C)

    def propagate_fine(start):
        current = start
        for step_index in range(STEPS):
            current = implicit_solve(current, fine_faces, fine_diag, COUPLING, fine_weights)
        return current

    fine_end = lax.map(propagate_fine, states)
    carried = jnp.zeros_like(restrict(states[0]))
    outputs = []
    for index_now in range(SLICES):
        stepped = implicit_solve(carried, coarse_faces, coarse_diag, 0.5 * COUPLING, coarse_weights)
        outputs.append(fine_end[index_now] + prolong(stepped))
        if index_now + 1 < SLICES:
            carried = stepped + (restrict(fine_end[index_now]) - restrict(states[index_now + 1]))
    return jnp.stack(outputs)
```

```python
import functools
import math

import jax
import jax.numpy as jnp
from jax import lax
from jax.experimental import pallas as pl
from jax.experimental.pallas import tpu as pltpu
from jax.sharding import PartitionSpec as P

STEPS = 2
SWEEPS = 3
SWEEPS_C = 2

COUPLING = 1.0
SPREAD = 0.85
H = SWEEPS
HC = SWEEPS_C
MESH = pl.DeviceIdType.MESH


def chebyshev_weights(count):
    return [
        1.0 / (1.0 + SPREAD * math.cos(math.pi * (2 * index_now + 1) / (2 * count)))
        for index_now in range(count)
    ]


def down(v, axis):
    return pltpu.roll(v, 1, axis)


def up(v, axis):
    return pltpu.roll(v, v.shape[axis] - 1, axis)


def coefficients(k_ref, bx, by, bz, inv, layers, coupling, keep):
    first, last = layers
    shape = k_ref.shape[1:]
    at_x = lax.broadcasted_iota(jnp.int32, shape, 0)
    at_y = lax.broadcasted_iota(jnp.int32, shape, 1)
    half = 0.5 * coupling
    for l in range(first, last):
        k = k_ref[l]
        x_lo = jnp.where(at_x == 0, 0.0, down(k, 0))
        x_hi = jnp.where(at_x == shape[0] - 1, 0.0, up(k, 0))
        y_lo = jnp.where(at_y == 0, 0.0, down(k, 1))
        y_hi = jnp.where(at_y == shape[1] - 1, 0.0, up(k, 1))
        bx[l] = jnp.where(at_x == 0, 0.0, half * (k + x_lo))
        by[l] = jnp.where(at_y == 0, 0.0, half * (k + y_lo))
        bz[l] = half * (k + k_ref[l - 1])
        diag = 1.0 + half * (
            6.0 * k + (x_lo + x_hi) + (y_lo + y_hi) + (k_ref[l - 1] + k_ref[l + 1])
        )
        inv[l] = keep(l) / diag
    bz[last] = half * (k_ref[last] + k_ref[last - 1])


def sweep(src, source, dst, bx, by, bz, inv, layers, weight):
    first, last = layers
    for l in range(first, last):
        w = src[l]
        b_y = by[l]
        b_x = bx[l]
        total = (
            source[l]
            + (b_y * down(w, 1) + up(b_y * w, 1))
            + (b_x * down(w, 0) + up(b_x * w, 0))
            + (bz[l] * src[l - 1] + bz[l + 1] * src[l + 1])
        )
        dst[l] = (1.0 - weight) * w + (weight * inv[l]) * total


def restricted(field, first, pairs, tmp, matrix):
    rows = tmp.shape[1]
    sums = [field[first + 2 * j] + field[first + 2 * j + 1] for j in range(pairs)]
    narrow = lax.dot_general(
        jnp.concatenate(sums, axis=0),
        matrix,
        (((1,), (0,)), ((), ())),
        precision=lax.Precision.HIGHEST,
        preferred_element_type=jnp.float32,
    )
    half = rows // 2
    out = []
    for j in range(pairs):
        tmp[j] = narrow[j * rows : (j + 1) * rows]
        out.append(tmp[j, pl.ds(0, half, 2), :] + tmp[j, pl.ds(1, half, 2), :])
    return out


def kernel(
    cut_count, gz_count, layers,
    s_in, k_in, out,
    s1, s2, wa, wb, k, bx, by, bz, inv, tmp,
    kc, cx, cy, cz, cinv, car, ca, cb, rs, rs_next, outgoing,
    load_sem, send_sem, recv_sem,
):
    cut = lax.axis_index("cuts")
    gz = lax.axis_index("gz")
    has_lo, has_hi = gz > 0, gz < gz_count - 1
    has_prev, has_next = cut > 0, cut < cut_count - 1
    coarse = layers // 2
    own = pl.ds(H, layers)
    own_c = pl.ds(HC, coarse)

    load_s = pltpu.make_async_copy(s_in.at[0], s1.at[own], load_sem.at[0])
    load_k = pltpu.make_async_copy(k_in, k.at[own], load_sem.at[1])
    load_k.start()
    load_s.start()

    barrier = pltpu.get_barrier_semaphore()
    n_z = has_lo.astype(jnp.int32) + has_hi.astype(jnp.int32)
    n_c = has_prev.astype(jnp.int32) + has_next.astype(jnp.int32)
    for dc, c_ok in ((0, None), (-1, has_prev), (1, has_next)):
        for dz, z_ok in ((-1, has_lo), (1, has_hi), (0, None)):
            if dc == 0 and dz == 0:
                continue
            ok = z_ok if c_ok is None else (c_ok if z_ok is None else c_ok & z_ok)

            @pl.when(ok)
            def _(dc=dc, dz=dz):
                pl.semaphore_signal(
                    barrier, inc=1, device_id=(cut + dc, gz + dz), device_id_type=MESH
                )

    zero_halo = jnp.zeros((H,) + s1.shape[1:], jnp.float32)
    zero_c = jnp.zeros((HC,) + car.shape[1:], jnp.float32)

    @pl.when(jnp.logical_not(has_lo))
    def _():
        for ref in (s1, s2, k):
            ref[pl.ds(0, H)] = zero_halo
        for ref in (kc, car):
            ref[pl.ds(0, HC)] = zero_c

    @pl.when(jnp.logical_not(has_hi))
    def _():
        for ref in (s1, s2, k):
            ref[pl.ds(H + layers, H)] = zero_halo
        for ref in (kc, car):
            ref[pl.ds(HC + coarse, HC)] = zero_c

    pl.semaphore_wait(barrier, n_z + n_c * (1 + n_z))

    def remote(src, dst, index, dc, dz):
        return pltpu.make_async_remote_copy(
            src_ref=src,
            dst_ref=dst,
            send_sem=send_sem.at[index],
            recv_sem=recv_sem.at[index],
            device_id=(cut + dc, gz + dz),
            device_id_type=MESH,
        )

    class Pair:
        def __init__(self, up_src, up_dst, down_src, down_dst, index):
            self.above = remote(up_src, up_dst, index, 0, 1)
            self.below = remote(down_src, down_dst, index + 1, 0, -1)

        def each(self, when_above, act_above, when_below, act_below):
            pl.when(when_above)(act_above)
            pl.when(when_below)(act_below)

        def start(self):
            self.each(has_hi, self.above.start, has_lo, self.below.start)

        def wait_recv(self):
            self.each(has_lo, self.above.wait_recv, has_hi, self.below.wait_recv)

        def wait_send(self):
            self.each(has_hi, self.above.wait_send, has_lo, self.below.wait_send)

    lo, hi = pl.ds(0, H), pl.ds(H + layers, H)
    first, final = pl.ds(0, H), pl.ds(layers - H, H)
    k_pair = Pair(k_in.at[final], k.at[lo], k_in.at[first], k.at[hi], 0)
    s_pair = Pair(s_in.at[0, final], s1.at[lo], s_in.at[0, first], s1.at[hi], 2)
    k_pair.start()
    s_pair.start()

    load_k.wait()
    load_s.wait()

    fine_y = s1.shape[2]
    row = lax.broadcasted_iota(jnp.int32, (fine_y, fine_y // 2), 0)
    col = lax.broadcasted_iota(jnp.int32, (fine_y, fine_y // 2), 1)
    gather = jnp.where((row == 2 * col) | (row == 2 * col + 1), 0.125, 0.0)

    for j, value in enumerate(restricted(s1, H, coarse, tmp, gather)):
        rs[j] = value
    for j, value in enumerate(restricted(k, H, coarse, tmp, gather)):
        kc[HC + j] = value
    rs_copy = remote(rs, rs_next, 6, -1, 0)
    pl.when(has_prev)(rs_copy.start)
    kc_lo, kc_hi = pl.ds(0, HC), pl.ds(HC + coarse, HC)
    kc_pair = Pair(
        kc.at[pl.ds(coarse, HC)], kc.at[kc_lo], kc.at[pl.ds(HC, HC)], kc.at[kc_hi], 4
    )
    kc_pair.start()

    lo_keep = jnp.where(has_lo, 1.0, 0.0)
    hi_keep = jnp.where(has_hi, 1.0, 0.0)

    def keep_in(halo, count):
        def keep(l):
            return lo_keep if l < halo else (hi_keep if l >= halo + count else 1.0)

        return keep

    k_pair.wait_recv()
    total = layers + 2 * H
    coefficients(k, bx, by, bz, inv, (1, total - 1), COUPLING, keep_in(H, layers))

    weights = chebyshev_weights(SWEEPS)

    def step(source, result):
        src = source
        for j, weight in enumerate(weights):
            dst = result if j == SWEEPS - 1 else (wa, wb)[j % 2]
            sweep(
                src, source, dst, bx, by, bz, inv, (j + 1, total - 1 - j), weight
            )
            src = dst

    s_pair.wait_recv()
    step(s1, s2)

    b_pair = Pair(
        s2.at[pl.ds(layers, H)], s2.at[lo], s2.at[pl.ds(H, H)], s2.at[hi], 7
    )
    b_pair.start()

    kc_pair.wait_recv()
    total_c = coarse + 2 * HC
    coefficients(
        kc, cx, cy, cz, cinv, (1, total_c - 1), 0.5 * COUPLING, keep_in(HC, coarse)
    )

    b_pair.wait_recv()
    step(s2, s1)

    coarse_weights = chebyshev_weights(SWEEPS_C)

    def send_on(dz, index, place):
        return remote(outgoing, car.at[place], index, 1, dz)

    to_same = send_on(0, 9, own_c)
    to_above = send_on(1, 10, kc_lo)
    to_below = send_on(-1, 11, kc_hi)

    @pl.when(has_next)
    def _():
        rs_copy.wait_recv()
        for j, value in enumerate(restricted(s1, H, coarse, tmp, gather)):
            outgoing[j] = value - rs_next[j]

    @pl.when(has_prev)
    def _():
        to_same.wait_recv()
        pl.when(has_lo)(to_above.wait_recv)
        pl.when(has_hi)(to_below.wait_recv)
        src = car
        for j, weight in enumerate(coarse_weights):
            dst = (ca, cb)[j % 2]
            sweep(
                src, car, dst, cx, cy, cz, cinv, (j + 1, total_c - 1 - j), weight
            )
            src = dst
        stepped = src

        @pl.when(has_next)
        def _():
            outgoing[...] = outgoing[...] + stepped[own_c]

        row_s = lax.broadcasted_iota(jnp.int32, (fine_y // 2, fine_y), 0)
        col_s = lax.broadcasted_iota(jnp.int32, (fine_y // 2, fine_y), 1)
        spread = jnp.where((col_s == 2 * row_s) | (col_s == 2 * row_s + 1), 1.0, 0.0)
        rows = tmp.shape[1]
        for j in range(coarse):
            part = stepped[HC + j]
            tmp[j, pl.ds(0, rows // 2, 2), :] = part
            tmp[j, pl.ds(1, rows // 2, 2), :] = part
        wide = lax.dot_general(
            jnp.concatenate([tmp[j] for j in range(coarse)], axis=0),
            spread,
            (((1,), (0,)), ((), ())),
            precision=lax.Precision.HIGHEST,
            preferred_element_type=jnp.float32,
        )
        for l in range(layers):
            out[0, l] = s1[H + l] + wide[(l // 2) * rows : (l // 2 + 1) * rows]

    @pl.when(has_next)
    def _():
        to_same.start()
        pl.when(has_hi)(to_above.start)
        pl.when(has_lo)(to_below.start)

    @pl.when(jnp.logical_not(has_prev))
    def _():
        out[0] = s1[own]

    k_pair.wait_send()
    s_pair.wait_send()
    kc_pair.wait_send()
    b_pair.wait_send()
    pl.when(has_prev)(rs_copy.wait_send)

    @pl.when(has_next)
    def _():
        to_same.wait_send()
        pl.when(has_hi)(to_above.wait_send)
        pl.when(has_lo)(to_below.wait_send)


def shards(states, conduct):
    cut_count, gz_count = lax.axis_size("cuts"), lax.axis_size("gz")
    layers, nx, ny = conduct.shape
    fine = pltpu.VMEM((layers + 2 * H, nx, ny), jnp.float32)
    coarse = pltpu.VMEM((layers // 2 + 2 * HC, nx // 2, ny // 2), jnp.float32)
    small = pltpu.VMEM((layers // 2, nx // 2, ny // 2), jnp.float32)
    return pl.pallas_call(
        functools.partial(kernel, cut_count, gz_count, layers),
        out_shape=jax.ShapeDtypeStruct(states.shape, jnp.float32),
        in_specs=[pl.BlockSpec(memory_space=pl.ANY)] * 2,
        out_specs=pl.BlockSpec(memory_space=pltpu.VMEM),
        scratch_shapes=[fine] * 9
        + [pltpu.VMEM((layers // 2, nx, ny // 2), jnp.float32)]
        + [coarse] * 8
        + [small] * 3
        + [
            pltpu.SemaphoreType.DMA((2,)),
            pltpu.SemaphoreType.DMA((12,)),
            pltpu.SemaphoreType.DMA((12,)),
        ],
        compiler_params=pltpu.CompilerParams(collective_id=0, has_side_effects=True),
        name="parareal",
    )(states, conduct)


def solution(mesh):
    in_specs = (P("cuts", "gz", None, None), P("gz", None, None))
    out_specs = P("cuts", "gz", None, None)
    return jax.shard_map(shards, mesh=mesh, in_specs=in_specs, out_specs=out_specs, check_vma=False)
```

```python
import functools
import math

import jax
import jax.numpy as jnp
from jax import lax
from jax.experimental import pallas as pl
from jax.experimental.pallas import tpu as pltpu
from jax.sharding import PartitionSpec as P

STEPS = 2
SWEEPS = 3
SWEEPS_C = 2

COUPLING = 1.0
SPREAD = 0.85
H = SWEEPS
HC = SWEEPS_C
MESH = pl.DeviceIdType.MESH


def chebyshev_weights(count):
    return [
        1.0 / (1.0 + SPREAD * math.cos(math.pi * (2 * index_now + 1) / (2 * count)))
        for index_now in range(count)
    ]


def down(v, axis):
    return pltpu.roll(v, 1, axis)


def up(v, axis):
    return pltpu.roll(v, v.shape[axis] - 1, axis)


def coefficient_layer(k_ref, bx, by, inv, l, coupling, keep):
    shape = k_ref.shape[1:]
    at_x = lax.broadcasted_iota(jnp.int32, shape, 0)
    at_y = lax.broadcasted_iota(jnp.int32, shape, 1)
    half = 0.5 * coupling
    k = k_ref[l]
    x_lo = jnp.where(at_x == 0, 0.0, down(k, 0))
    x_hi = jnp.where(at_x == shape[0] - 1, 0.0, up(k, 0))
    y_lo = jnp.where(at_y == 0, 0.0, down(k, 1))
    y_hi = jnp.where(at_y == shape[1] - 1, 0.0, up(k, 1))
    bx[l] = jnp.where(at_x == 0, 0.0, half * (k + x_lo))
    by[l] = jnp.where(at_y == 0, 0.0, half * (k + y_lo))
    diag = 1.0 + half * (
        6.0 * k + (x_lo + x_hi) + (y_lo + y_hi) + (k_ref[l - 1] + k_ref[l + 1])
    )
    inv[l] = keep / diag


def sweep_layer(src, source, dst, bx, by, bz, inv, l, weight):
    w = src[l]
    b_y = by[l]
    b_x = bx[l]
    total = (
        source[l]
        + (b_y * down(w, 1) + up(b_y * w, 1))
        + (b_x * down(w, 0) + up(b_x * w, 0))
        + (bz[l] * src[l - 1] + bz[l + 1] * src[l + 1])
    )
    dst[l] = (1.0 - weight) * w + (weight * inv[l]) * total


def times_exact(value, matrix):
    high = value.astype(jnp.bfloat16)
    rest = value - high.astype(jnp.float32)
    middle = rest.astype(jnp.bfloat16)
    low = (rest - middle.astype(jnp.float32)).astype(jnp.bfloat16)
    count = value.shape[0]
    parts = lax.dot_general(
        jnp.concatenate([high, middle, low], axis=0),
        matrix.astype(jnp.bfloat16),
        (((1,), (0,)), ((), ())),
        preferred_element_type=jnp.float32,
    )
    return parts[:count] + (parts[count : 2 * count] + parts[2 * count :])


class Grid:
    def __init__(self, halo, count, k, bx, by, bz, inv, coupling, keeps):
        self.halo, self.count = halo, count
        self.k, self.bx, self.by, self.bz, self.inv = k, bx, by, bz, inv
        self.coupling = coupling
        self.keeps = keeps

    def depth(self, l):
        return max(self.halo - l, l - (self.halo + self.count - 1))

    def keep(self, l):
        return self.keeps[0] if l < self.halo else (self.keeps[1] if l >= self.halo + self.count else 1.0)

    def coefficients(self, depth):
        total = self.count + 2 * self.halo
        for l in range(1, total):
            if max(0, self.depth(l), self.depth(l - 1)) == depth:
                self.bz[l] = 0.5 * self.coupling * (self.k[l] + self.k[l - 1])
        for l in range(1, total - 1):
            if max(0, self.depth(l) + 1) == depth:
                coefficient_layer(
                    self.k, self.bx, self.by, self.inv, l, self.coupling, self.keep(l)
                )

    def sweeps(self, buffers, weights, depth):
        source = buffers[0]
        sweeps = len(weights)
        for j, weight in enumerate(weights):
            for l in range(j + 1, self.count + 2 * self.halo - 1 - j):
                if self.depth(l) > sweeps - 1 - j:
                    continue
                if max(0, self.depth(l) + j + 1) == depth:
                    sweep_layer(
                        buffers[j], source, buffers[j + 1],
                        self.bx, self.by, self.bz, self.inv, l, weight,
                    )


def restricted(field, first, pairs, tmp, matrix):
    rows = tmp.shape[1]
    sums = [field[first + 2 * j] + field[first + 2 * j + 1] for j in range(pairs)]
    narrow = times_exact(jnp.concatenate(sums, axis=0), matrix)
    half = rows // 2
    out = []
    for j in range(pairs):
        tmp[j] = narrow[j * rows : (j + 1) * rows]
        out.append(tmp[j, pl.ds(0, half, 2), :] + tmp[j, pl.ds(1, half, 2), :])
    return out


def kernel(
    cut_count, gz_count, layers,
    s_in, k_in, out,
    s1, s2, wa, wb, k, bx, by, bz, inv, tmp,
    kc, cx, cy, cz, cinv, car, ca, cb, rs, rs_next, outgoing,
    load_sem, send_sem, recv_sem,
):
    cut = lax.axis_index("cuts")
    gz = lax.axis_index("gz")
    has_lo, has_hi = gz > 0, gz < gz_count - 1
    has_prev, has_next = cut > 0, cut < cut_count - 1
    coarse = layers // 2
    own = pl.ds(H, layers)
    own_c = pl.ds(HC, coarse)

    load_s = pltpu.make_async_copy(s_in.at[0], s1.at[own], load_sem.at[0])
    load_k = pltpu.make_async_copy(k_in, k.at[own], load_sem.at[1])
    load_k.start()
    load_s.start()

    barrier = pltpu.get_barrier_semaphore()
    n_z = has_lo.astype(jnp.int32) + has_hi.astype(jnp.int32)
    n_c = has_prev.astype(jnp.int32) + has_next.astype(jnp.int32)
    for dc, dz, ok in ((0, -1, has_lo), (0, 1, has_hi), (-1, 0, has_prev), (1, 0, has_next)):

        @pl.when(ok)
        def _(dc=dc, dz=dz):
            pl.semaphore_signal(
                barrier, inc=1, device_id=(cut + dc, gz + dz), device_id_type=MESH
            )

    zero_halo = jnp.zeros((H,) + s1.shape[1:], jnp.float32)
    zero_c = jnp.zeros((HC,) + car.shape[1:], jnp.float32)

    @pl.when(jnp.logical_not(has_lo))
    def _():
        for ref in (s1, s2, k):
            ref[pl.ds(0, H)] = zero_halo
        for ref in (kc, car):
            ref[pl.ds(0, HC)] = zero_c

    @pl.when(jnp.logical_not(has_hi))
    def _():
        for ref in (s1, s2, k):
            ref[pl.ds(H + layers, H)] = zero_halo
        for ref in (kc, car):
            ref[pl.ds(HC + coarse, HC)] = zero_c

    pl.semaphore_wait(barrier, n_z + n_c)

    def remote(src, dst, index, dc, dz):
        return pltpu.make_async_remote_copy(
            src_ref=src,
            dst_ref=dst,
            send_sem=send_sem.at[index],
            recv_sem=recv_sem.at[index],
            device_id=(cut + dc, gz + dz),
            device_id_type=MESH,
        )

    class Pair:
        def __init__(self, up_src, up_dst, down_src, down_dst, index):
            self.above = remote(up_src, up_dst, index, 0, 1)
            self.below = remote(down_src, down_dst, index + 1, 0, -1)

        def each(self, when_above, act_above, when_below, act_below):
            pl.when(when_above)(act_above)
            pl.when(when_below)(act_below)

        def start(self):
            self.each(has_hi, self.above.start, has_lo, self.below.start)

        def wait_recv(self):
            self.each(has_lo, self.above.wait_recv, has_hi, self.below.wait_recv)

        def wait_send(self):
            self.each(has_hi, self.above.wait_send, has_lo, self.below.wait_send)

    k_pairs, s_pairs, b_pairs = [], [], []
    for d in range(1, H + 1):
        near, far = layers - d, d - 1
        low, high = H - d, H + layers + d - 1
        k_pairs.append(
            Pair(k_in.at[near], k.at[low], k_in.at[far], k.at[high], 4 * (d - 1))
        )
        s_pairs.append(
            Pair(s_in.at[0, near], s1.at[low], s_in.at[0, far], s1.at[high], 4 * (d - 1) + 2)
        )
        b_pairs.append(
            Pair(s2.at[H + near], s2.at[low], s2.at[H + far], s2.at[high], 4 * H + 2 * (d - 1))
        )
        k_pairs[-1].start()
        s_pairs[-1].start()
    after = 6 * H

    load_k.wait()
    load_s.wait()

    fine_y = s1.shape[2]
    row = lax.broadcasted_iota(jnp.int32, (fine_y, fine_y // 2), 0)
    col = lax.broadcasted_iota(jnp.int32, (fine_y, fine_y // 2), 1)
    gather = jnp.where((row == 2 * col) | (row == 2 * col + 1), 0.125, 0.0)

    for j, value in enumerate(restricted(s1, H, coarse, tmp, gather)):
        rs[j] = value
    rs_copy = remote(rs, rs_next, after, -1, 0)
    pl.when(has_prev)(rs_copy.start)
    kc_lo, kc_hi = pl.ds(0, HC), pl.ds(HC + coarse, HC)
    kc_pair = Pair(
        kc.at[pl.ds(coarse, HC)], kc.at[kc_lo], kc.at[pl.ds(HC, HC)], kc.at[kc_hi], after + 1
    )

    lo_keep = jnp.where(has_lo, 1.0, 0.0)
    hi_keep = jnp.where(has_hi, 1.0, 0.0)

    keeps = (lo_keep, hi_keep)
    fine = Grid(H, layers, k, bx, by, bz, inv, COUPLING, keeps)
    crude = Grid(HC, coarse, kc, cx, cy, cz, cinv, 0.5 * COUPLING, keeps)
    weights = chebyshev_weights(SWEEPS)
    coarse_weights = chebyshev_weights(SWEEPS_C)

    for d in range(H + 1):
        if d > 0:
            k_pairs[d - 1].wait_recv()
        fine.coefficients(d)
        if d > 0:
            s_pairs[d - 1].wait_recv()
        fine.sweeps((s1, wa, wb, s2), weights, d)

    for pair in b_pairs:
        pair.start()

    @pl.when(has_prev)
    def _():
        for j, value in enumerate(restricted(k, H, coarse, tmp, gather)):
            kc[HC + j] = value
        kc_pair.start()

    for d in range(H + 1):
        if d > 0:
            b_pairs[d - 1].wait_recv()
        fine.sweeps((s2, wa, wb, s1), weights, d)

    def send_on(dz, index, place):
        return remote(outgoing, car.at[place], index, 1, dz)

    to_same = send_on(0, after + 3, own_c)
    to_above = send_on(1, after + 4, kc_lo)
    to_below = send_on(-1, after + 5, kc_hi)

    @pl.when(has_next)
    def _():
        rs_copy.wait_recv()
        for j, value in enumerate(restricted(s1, H, coarse, tmp, gather)):
            outgoing[j] = value - rs_next[j]

    @pl.when(has_prev)
    def _():
        kc_pair.wait_recv()
        for d in range(HC + 1):
            crude.coefficients(d)
        to_same.wait_recv()
        pl.when(has_lo)(to_above.wait_recv)
        pl.when(has_hi)(to_below.wait_recv)
        for d in range(HC + 1):
            crude.sweeps((car, ca, cb), coarse_weights, d)
        stepped = cb

        @pl.when(has_next)
        def _():
            outgoing[...] = outgoing[...] + stepped[own_c]

        row_s = lax.broadcasted_iota(jnp.int32, (fine_y // 2, fine_y), 0)
        col_s = lax.broadcasted_iota(jnp.int32, (fine_y // 2, fine_y), 1)
        spread = jnp.where((col_s == 2 * row_s) | (col_s == 2 * row_s + 1), 1.0, 0.0)
        rows = tmp.shape[1]
        for j in range(coarse):
            part = stepped[HC + j]
            tmp[j, pl.ds(0, rows // 2, 2), :] = part
            tmp[j, pl.ds(1, rows // 2, 2), :] = part
        wide = times_exact(jnp.concatenate([tmp[j] for j in range(coarse)], axis=0), spread)
        for l in range(layers):
            out[0, l] = s1[H + l] + wide[(l // 2) * rows : (l // 2 + 1) * rows]

    @pl.when(has_next)
    def _():
        to_same.start()
        pl.when(has_hi)(to_above.start)
        pl.when(has_lo)(to_below.start)

    @pl.when(jnp.logical_not(has_prev))
    def _():
        out[0] = s1[own]

    for pair in k_pairs + s_pairs + b_pairs:
        pair.wait_send()

    @pl.when(has_prev)
    def _():
        kc_pair.wait_send()
        rs_copy.wait_send()

    @pl.when(has_next)
    def _():
        to_same.wait_send()
        pl.when(has_hi)(to_above.wait_send)
        pl.when(has_lo)(to_below.wait_send)


def shards(states, conduct):
    cut_count, gz_count = lax.axis_size("cuts"), lax.axis_size("gz")
    layers, nx, ny = conduct.shape
    fine = pltpu.VMEM((layers + 2 * H, nx, ny), jnp.float32)
    coarse = pltpu.VMEM((layers // 2 + 2 * HC, nx // 2, ny // 2), jnp.float32)
    small = pltpu.VMEM((layers // 2, nx // 2, ny // 2), jnp.float32)
    return pl.pallas_call(
        functools.partial(kernel, cut_count, gz_count, layers),
        out_shape=pltpu.VMEM(states.shape, jnp.float32),
        in_specs=[pl.BlockSpec(memory_space=pl.ANY)] * 2,
        out_specs=pl.BlockSpec(memory_space=pltpu.VMEM),
        scratch_shapes=[fine] * 9
        + [pltpu.VMEM((layers // 2, nx, ny // 2), jnp.float32)]
        + [coarse] * 8
        + [small] * 3
        + [
            pltpu.SemaphoreType.DMA((2,)),
            pltpu.SemaphoreType.DMA((6 * H + 6,)),
            pltpu.SemaphoreType.DMA((6 * H + 6,)),
        ],
        compiler_params=pltpu.CompilerParams(collective_id=0, has_side_effects=True),
        name="parareal",
    )(states, conduct)


def solution(mesh):
    in_specs = (P("cuts", "gz", None, None), P("gz", None, None))
    out_specs = P("cuts", "gz", None, None)
    return jax.shard_map(shards, mesh=mesh, in_specs=in_specs, out_specs=out_specs, check_vma=False)
```

```python
import functools
import math

import jax
import jax.numpy as jnp
from jax import lax
from jax.experimental import pallas as pl
from jax.experimental.pallas import tpu as pltpu
from jax.sharding import PartitionSpec as P

STEPS = 2
SWEEPS = 3
SWEEPS_C = 2

COUPLING = 1.0
SPREAD = 0.85
H = SWEEPS
HC = SWEEPS_C
MESH = pl.DeviceIdType.MESH


def chebyshev_weights(count):
    return [
        1.0 / (1.0 + SPREAD * math.cos(math.pi * (2 * index_now + 1) / (2 * count)))
        for index_now in range(count)
    ]


def down(v, axis):
    return pltpu.roll(v, 1, axis)


def up(v, axis):
    return pltpu.roll(v, v.shape[axis] - 1, axis)


def coefficient_layer(k_ref, bx, by, inv, l, coupling, keep):
    shape = k_ref.shape[1:]
    at_x = lax.broadcasted_iota(jnp.int32, shape, 0)
    at_y = lax.broadcasted_iota(jnp.int32, shape, 1)
    half = 0.5 * coupling
    k = k_ref[l]
    x_lo = jnp.where(at_x == 0, 0.0, down(k, 0))
    x_hi = jnp.where(at_x == shape[0] - 1, 0.0, up(k, 0))
    y_lo = jnp.where(at_y == 0, 0.0, down(k, 1))
    y_hi = jnp.where(at_y == shape[1] - 1, 0.0, up(k, 1))
    bx[l] = jnp.where(at_x == 0, 0.0, half * (k + x_lo))
    by[l] = jnp.where(at_y == 0, 0.0, half * (k + y_lo))
    diag = 1.0 + half * (
        6.0 * k + (x_lo + x_hi) + (y_lo + y_hi) + (k_ref[l - 1] + k_ref[l + 1])
    )
    inv[l] = keep / diag


def sweep_layer(src, source, dst, bx, by, bz, inv, l, weight):
    w = src[l]
    b_y = by[l]
    b_x = bx[l]
    total = (
        source[l]
        + (b_y * down(w, 1) + up(b_y * w, 1))
        + (b_x * down(w, 0) + up(b_x * w, 0))
        + (bz[l] * src[l - 1] + bz[l + 1] * src[l + 1])
    )
    dst[l] = (1.0 - weight) * w + (weight * inv[l]) * total


def times_exact(value, matrix):
    high = value.astype(jnp.bfloat16)
    rest = value - high.astype(jnp.float32)
    middle = rest.astype(jnp.bfloat16)
    low = (rest - middle.astype(jnp.float32)).astype(jnp.bfloat16)
    count = value.shape[0]
    parts = lax.dot_general(
        jnp.concatenate([high, middle, low], axis=0),
        matrix.astype(jnp.bfloat16),
        (((1,), (0,)), ((), ())),
        preferred_element_type=jnp.float32,
    )
    return parts[:count] + (parts[count : 2 * count] + parts[2 * count :])


class Grid:
    def __init__(self, halo, count, k, bx, by, bz, inv, coupling, keeps):
        self.halo, self.count = halo, count
        self.k, self.bx, self.by, self.bz, self.inv = k, bx, by, bz, inv
        self.coupling = coupling
        self.keeps = keeps

    def depth(self, l):
        return max(self.halo - l, l - (self.halo + self.count - 1))

    def keep(self, l):
        return self.keeps[0] if l < self.halo else (self.keeps[1] if l >= self.halo + self.count else 1.0)

    def coefficients(self, depth):
        total = self.count + 2 * self.halo
        for l in range(1, total):
            if max(0, self.depth(l), self.depth(l - 1)) == depth:
                self.bz[l] = 0.5 * self.coupling * (self.k[l] + self.k[l - 1])
        for l in range(1, total - 1):
            if max(0, self.depth(l) + 1) == depth:
                coefficient_layer(
                    self.k, self.bx, self.by, self.inv, l, self.coupling, self.keep(l)
                )

    def sweeps(self, buffers, weights, depth):
        source = buffers[0]
        sweeps = len(weights)
        for j, weight in enumerate(weights):
            for l in range(j + 1, self.count + 2 * self.halo - 1 - j):
                if self.depth(l) > sweeps - 1 - j:
                    continue
                if max(0, self.depth(l) + j + 1) == depth:
                    sweep_layer(
                        buffers[j], source, buffers[j + 1],
                        self.bx, self.by, self.bz, self.inv, l, weight,
                    )


def restricted(field, first, pairs, tmp, matrix):
    rows = tmp.shape[1]
    sums = [field[first + 2 * j] + field[first + 2 * j + 1] for j in range(pairs)]
    narrow = times_exact(jnp.concatenate(sums, axis=0), matrix)
    half = rows // 2
    out = []
    for j in range(pairs):
        tmp[j] = narrow[j * rows : (j + 1) * rows]
        out.append(tmp[j, pl.ds(0, half, 2), :] + tmp[j, pl.ds(1, half, 2), :])
    return out


def kernel(
    cut_count, gz_count, layers,
    s_in, k_in, out,
    s1, s2, wa, wb, end, k, bx, by, bz, inv, tmp,
    kc, cx, cy, cz, cinv, car, ca, cb, rs, rs_next, outgoing,
    load_sem, send_sem, recv_sem,
):
    cut = lax.axis_index("cuts")
    gz = lax.axis_index("gz")
    has_lo, has_hi = gz > 0, gz < gz_count - 1
    has_prev, has_next = cut > 0, cut < cut_count - 1
    coarse = layers // 2
    own = pl.ds(H, layers)
    own_c = pl.ds(HC, coarse)

    load_s = pltpu.make_async_copy(s_in.at[0], s1.at[own], load_sem.at[0])
    load_k = pltpu.make_async_copy(k_in, k.at[own], load_sem.at[1])
    load_k.start()
    load_s.start()

    barrier = pltpu.get_barrier_semaphore()
    n_z = has_lo.astype(jnp.int32) + has_hi.astype(jnp.int32)
    n_c = has_prev.astype(jnp.int32) + has_next.astype(jnp.int32)
    for dc, dz, ok in ((0, -1, has_lo), (0, 1, has_hi), (-1, 0, has_prev), (1, 0, has_next)):

        @pl.when(ok)
        def _(dc=dc, dz=dz):
            pl.semaphore_signal(
                barrier, inc=1, device_id=(cut + dc, gz + dz), device_id_type=MESH
            )

    zero_halo = jnp.zeros((H,) + s1.shape[1:], jnp.float32)
    zero_c = jnp.zeros((HC,) + car.shape[1:], jnp.float32)

    @pl.when(jnp.logical_not(has_lo))
    def _():
        for ref in (s1, s2, k):
            ref[pl.ds(0, H)] = zero_halo
        for ref in (kc, car):
            ref[pl.ds(0, HC)] = zero_c

    @pl.when(jnp.logical_not(has_hi))
    def _():
        for ref in (s1, s2, k):
            ref[pl.ds(H + layers, H)] = zero_halo
        for ref in (kc, car):
            ref[pl.ds(HC + coarse, HC)] = zero_c

    load_k.wait()
    load_s.wait()
    pl.semaphore_wait(barrier, n_z + n_c)

    def remote(src, dst, index, dc, dz):
        return pltpu.make_async_remote_copy(
            src_ref=src,
            dst_ref=dst,
            send_sem=send_sem.at[index],
            recv_sem=recv_sem.at[index],
            device_id=(cut + dc, gz + dz),
            device_id_type=MESH,
        )

    class Pair:
        def __init__(self, up_src, up_dst, down_src, down_dst, index):
            self.above = remote(up_src, up_dst, index, 0, 1)
            self.below = remote(down_src, down_dst, index + 1, 0, -1)

        def each(self, when_above, act_above, when_below, act_below):
            pl.when(when_above)(act_above)
            pl.when(when_below)(act_below)

        def start(self, hi=has_hi, lo=has_lo):
            self.each(hi, self.above.start, lo, self.below.start)

        def wait_recv(self, lo=has_lo, hi=has_hi):
            self.each(lo, self.above.wait_recv, hi, self.below.wait_recv)

        def wait_send(self, hi=has_hi, lo=has_lo):
            self.each(hi, self.above.wait_send, lo, self.below.wait_send)

    k_pairs, s_pairs, b_pairs = [], [], []
    for d in range(1, H + 1):
        near, far = layers - d, d - 1
        low, high = H - d, H + layers + d - 1
        k_pairs.append(
            Pair(k.at[H + near], k.at[low], k.at[H + far], k.at[high], 4 * (d - 1))
        )
        s_pairs.append(
            Pair(s1.at[H + near], s1.at[low], s1.at[H + far], s1.at[high], 4 * (d - 1) + 2)
        )
        b_pairs.append(
            Pair(s2.at[H + near], s2.at[low], s2.at[H + far], s2.at[high], 4 * H + 2 * (d - 1))
        )
    after = 6 * H

    if cut_count > 1:
        odd = lax.rem(gz, 2) == 1
        even = jnp.logical_not(odd)
        outer_hi, outer_lo = has_hi & (even | has_prev), has_lo & (odd | has_prev)
        pass_hi, pass_lo = has_hi & odd & (cut == 1), has_lo & even & (cut == 1)
        take_hi, take_lo = has_hi & odd & (cut == 0), has_lo & even & (cut == 0)
        top = 2 * H + layers - 1
        pass_low = remote(k.at[0], k.at[0], after + 6, -1, 0)
        pass_high = remote(k.at[top], k.at[top], after + 7, -1, 0)
        late_hi, late_lo = (
            outer_hi & jnp.logical_not(pass_hi),
            outer_lo & jnp.logical_not(pass_lo),
        )
    else:
        outer_hi, outer_lo, late_hi, late_lo = has_hi, has_lo, has_hi, has_lo

    k_pairs[-1].start(outer_hi, outer_lo)
    for d in range(H):
        if d < H - 1:
            k_pairs[d].start()
        s_pairs[d].start()

    fine_y = s1.shape[2]
    row = lax.broadcasted_iota(jnp.int32, (fine_y, fine_y // 2), 0)
    col = lax.broadcasted_iota(jnp.int32, (fine_y, fine_y // 2), 1)
    gather = jnp.where((row == 2 * col) | (row == 2 * col + 1), 0.125, 0.0)

    for j, value in enumerate(restricted(s1, H, coarse, tmp, gather)):
        rs[j] = value
    rs_copy = remote(rs, rs_next, after, -1, 0)
    pl.when(has_prev)(rs_copy.start)
    kc_lo, kc_hi = pl.ds(0, HC), pl.ds(HC + coarse, HC)
    kc_pair = Pair(
        kc.at[pl.ds(coarse, HC)], kc.at[kc_lo], kc.at[pl.ds(HC, HC)], kc.at[kc_hi], after + 1
    )

    lo_keep = jnp.where(has_lo, 1.0, 0.0)
    hi_keep = jnp.where(has_hi, 1.0, 0.0)

    keeps = (lo_keep, hi_keep)
    fine = Grid(H, layers, k, bx, by, bz, inv, COUPLING, keeps)
    crude = Grid(HC, coarse, kc, cx, cy, cz, cinv, 0.5 * COUPLING, keeps)
    weights = chebyshev_weights(SWEEPS)
    coarse_weights = chebyshev_weights(SWEEPS_C)

    for d in range(H + 1):
        if d == 1 and cut_count > 1:

            @pl.when(pass_lo)
            def _():
                k_pairs[-1].above.wait_recv()
                pass_low.start()

            @pl.when(pass_hi)
            def _():
                k_pairs[-1].below.wait_recv()
                pass_high.start()

        if d == H:
            k_pairs[-1].wait_recv(late_lo, late_hi)
            if cut_count > 1:
                pl.when(take_lo)(pass_low.wait_recv)
                pl.when(take_hi)(pass_high.wait_recv)
        elif d > 0:
            k_pairs[d - 1].wait_recv()
        fine.coefficients(d)
        if d > 0:
            s_pairs[d - 1].wait_recv()
        fine.sweeps((s1, wa, wb, s2), weights, d)

    for pair in b_pairs:
        pair.start()

    @pl.when(has_prev)
    def _():
        for j, value in enumerate(restricted(k, H, coarse, tmp, gather)):
            kc[HC + j] = value
        kc_pair.start()

    for d in range(H + 1):
        if d > 0:
            b_pairs[d - 1].wait_recv()
        fine.sweeps((s2, wa, wb, end), weights, d)

    def send_on(dz, index, place):
        return remote(outgoing, car.at[place], index, 1, dz)

    to_same = send_on(0, after + 3, own_c)
    to_above = send_on(1, after + 4, kc_lo)
    to_below = send_on(-1, after + 5, kc_hi)

    @pl.when(has_next)
    def _():
        rs_copy.wait_recv()
        for j, value in enumerate(restricted(end, H, coarse, tmp, gather)):
            outgoing[j] = value - rs_next[j]

    @pl.when(has_prev)
    def _():
        kc_pair.wait_recv()
        for d in range(HC + 1):
            crude.coefficients(d)
        to_same.wait_recv()
        pl.when(has_lo)(to_above.wait_recv)
        pl.when(has_hi)(to_below.wait_recv)
        for d in range(HC + 1):
            crude.sweeps((car, ca, cb), coarse_weights, d)
        stepped = cb

        @pl.when(has_next)
        def _():
            outgoing[...] = outgoing[...] + stepped[own_c]

        row_s = lax.broadcasted_iota(jnp.int32, (fine_y // 2, fine_y), 0)
        col_s = lax.broadcasted_iota(jnp.int32, (fine_y // 2, fine_y), 1)
        spread = jnp.where((col_s == 2 * row_s) | (col_s == 2 * row_s + 1), 1.0, 0.0)
        rows = tmp.shape[1]
        for j in range(coarse):
            part = stepped[HC + j]
            tmp[j, pl.ds(0, rows // 2, 2), :] = part
            tmp[j, pl.ds(1, rows // 2, 2), :] = part
        wide = times_exact(jnp.concatenate([tmp[j] for j in range(coarse)], axis=0), spread)
        for l in range(layers):
            out[0, l] = end[H + l] + wide[(l // 2) * rows : (l // 2 + 1) * rows]

    @pl.when(has_next)
    def _():
        to_same.start()
        pl.when(has_hi)(to_above.start)
        pl.when(has_lo)(to_below.start)

    @pl.when(jnp.logical_not(has_prev))
    def _():
        out[0] = end[own]

    k_pairs[-1].wait_send(outer_hi, outer_lo)
    for pair in k_pairs[:-1] + s_pairs + b_pairs:
        pair.wait_send()
    if cut_count > 1:
        pl.when(pass_lo)(pass_low.wait_send)
        pl.when(pass_hi)(pass_high.wait_send)

    @pl.when(has_prev)
    def _():
        kc_pair.wait_send()
        rs_copy.wait_send()

    @pl.when(has_next)
    def _():
        to_same.wait_send()
        pl.when(has_hi)(to_above.wait_send)
        pl.when(has_lo)(to_below.wait_send)


def shards(states, conduct):
    cut_count, gz_count = lax.axis_size("cuts"), lax.axis_size("gz")
    layers, nx, ny = conduct.shape
    fine = pltpu.VMEM((layers + 2 * H, nx, ny), jnp.float32)
    coarse = pltpu.VMEM((layers // 2 + 2 * HC, nx // 2, ny // 2), jnp.float32)
    small = pltpu.VMEM((layers // 2, nx // 2, ny // 2), jnp.float32)
    return pl.pallas_call(
        functools.partial(kernel, cut_count, gz_count, layers),
        out_shape=pltpu.VMEM(states.shape, jnp.float32),
        in_specs=[pl.BlockSpec(memory_space=pl.ANY)] * 2,
        out_specs=pl.BlockSpec(memory_space=pltpu.VMEM),
        scratch_shapes=[fine] * 10
        + [pltpu.VMEM((layers // 2, nx, ny // 2), jnp.float32)]
        + [coarse] * 8
        + [small] * 3
        + [
            pltpu.SemaphoreType.DMA((2,)),
            pltpu.SemaphoreType.DMA((6 * H + 8,)),
            pltpu.SemaphoreType.DMA((6 * H + 8,)),
        ],
        compiler_params=pltpu.CompilerParams(collective_id=0, has_side_effects=True),
        name="parareal",
    )(states, conduct)


def solution(mesh):
    in_specs = (P("cuts", "gz", None, None), P("gz", None, None))
    out_specs = P("cuts", "gz", None, None)
    return jax.shard_map(shards, mesh=mesh, in_specs=in_specs, out_specs=out_specs, check_vma=False)
```

```python
import functools
import math

import jax
import jax.numpy as jnp
from jax import lax
from jax.experimental import pallas as pl
from jax.experimental.pallas import tpu as pltpu
from jax.sharding import PartitionSpec as P

STEPS = 2
SWEEPS = 3
SWEEPS_C = 2

COUPLING = 1.0
SPREAD = 0.85
H = SWEEPS
HC = SWEEPS_C
MESH = pl.DeviceIdType.MESH


def chebyshev_weights(count):
    return [
        1.0 / (1.0 + SPREAD * math.cos(math.pi * (2 * index_now + 1) / (2 * count)))
        for index_now in range(count)
    ]


def down(v, axis):
    return pltpu.roll(v, 1, axis)


def up(v, axis):
    return pltpu.roll(v, v.shape[axis] - 1, axis)


def coefficient_layer(k_ref, bx, by, inv, l, coupling, keep):
    shape = k_ref.shape[1:]
    at_x = lax.broadcasted_iota(jnp.int32, shape, 0)
    at_y = lax.broadcasted_iota(jnp.int32, shape, 1)
    half = 0.5 * coupling
    k = k_ref[l]
    x_lo = jnp.where(at_x == 0, 0.0, down(k, 0))
    x_hi = jnp.where(at_x == shape[0] - 1, 0.0, up(k, 0))
    y_lo = jnp.where(at_y == 0, 0.0, down(k, 1))
    y_hi = jnp.where(at_y == shape[1] - 1, 0.0, up(k, 1))
    bx[l] = jnp.where(at_x == 0, 0.0, half * (k + x_lo))
    by[l] = jnp.where(at_y == 0, 0.0, half * (k + y_lo))
    diag = 1.0 + half * (
        6.0 * k + (x_lo + x_hi) + (y_lo + y_hi) + (k_ref[l - 1] + k_ref[l + 1])
    )
    inv[l] = keep / diag


def sweep_layer(src, source, dst, bx, by, bz, inv, l, weight):
    w = src[l]
    b_y = by[l]
    b_x = bx[l]
    total = (
        source[l]
        + (b_y * down(w, 1) + up(b_y * w, 1))
        + (b_x * down(w, 0) + up(b_x * w, 0))
        + (bz[l] * src[l - 1] + bz[l + 1] * src[l + 1])
    )
    dst[l] = (1.0 - weight) * w + (weight * inv[l]) * total


def times_exact(value, matrix):
    high = value.astype(jnp.bfloat16)
    rest = value - high.astype(jnp.float32)
    middle = rest.astype(jnp.bfloat16)
    low = (rest - middle.astype(jnp.float32)).astype(jnp.bfloat16)
    count = value.shape[0]
    parts = lax.dot_general(
        jnp.concatenate([high, middle, low], axis=0),
        matrix.astype(jnp.bfloat16),
        (((1,), (0,)), ((), ())),
        preferred_element_type=jnp.float32,
    )
    return parts[:count] + (parts[count : 2 * count] + parts[2 * count :])


class Grid:
    def __init__(self, halo, count, k, bx, by, bz, inv, coupling, keeps):
        self.halo, self.count = halo, count
        self.k, self.bx, self.by, self.bz, self.inv = k, bx, by, bz, inv
        self.coupling = coupling
        self.keeps = keeps

    def depth(self, l):
        return max(self.halo - l, l - (self.halo + self.count - 1))

    def keep(self, l):
        return self.keeps[0] if l < self.halo else (self.keeps[1] if l >= self.halo + self.count else 1.0)

    def coefficients(self, depth):
        total = self.count + 2 * self.halo
        for l in range(1, total):
            if max(0, self.depth(l), self.depth(l - 1)) == depth:
                self.bz[l] = 0.5 * self.coupling * (self.k[l] + self.k[l - 1])
        for l in range(1, total - 1):
            if max(0, self.depth(l) + 1) == depth:
                coefficient_layer(
                    self.k, self.bx, self.by, self.inv, l, self.coupling, self.keep(l)
                )

    def sweeps(self, buffers, weights, depth):
        source = buffers[0]
        sweeps = len(weights)
        for j, weight in enumerate(weights):
            for l in range(j + 1, self.count + 2 * self.halo - 1 - j):
                if self.depth(l) > sweeps - 1 - j:
                    continue
                if max(0, self.depth(l) + j + 1) == depth:
                    sweep_layer(
                        buffers[j], source, buffers[j + 1],
                        self.bx, self.by, self.bz, self.inv, l, weight,
                    )


def restricted(field, first, pairs, tmp, matrix):
    rows = tmp.shape[1]
    sums = [field[first + 2 * j] + field[first + 2 * j + 1] for j in range(pairs)]
    narrow = times_exact(jnp.concatenate(sums, axis=0), matrix)
    half = rows // 2
    out = []
    for j in range(pairs):
        tmp[j] = narrow[j * rows : (j + 1) * rows]
        out.append(tmp[j, pl.ds(0, half, 2), :] + tmp[j, pl.ds(1, half, 2), :])
    return out


def kernel(
    cut_count, gz_count, layers,
    s_in, k_in, out,
    s1, s2, wa, wb, end, k, bx, by, bz, inv, tmp,
    kc, cx, cy, cz, cinv, car, ca, cb, rs, rs_next, outgoing,
    load_sem, send_sem, recv_sem,
):
    cut = lax.axis_index("cuts")
    gz = lax.axis_index("gz")
    has_lo, has_hi = gz > 0, gz < gz_count - 1
    has_prev, has_next = cut > 0, cut < cut_count - 1
    coarse = layers // 2
    own = pl.ds(H, layers)
    own_c = pl.ds(HC, coarse)

    load_s = pltpu.make_async_copy(s_in.at[0], s1.at[own], load_sem.at[0])
    load_k = pltpu.make_async_copy(k_in, k.at[own], load_sem.at[1])
    load_k.start()
    load_s.start()

    barrier = pltpu.get_barrier_semaphore()
    n_z = has_lo.astype(jnp.int32) + has_hi.astype(jnp.int32)
    n_c = has_prev.astype(jnp.int32) + has_next.astype(jnp.int32)
    for dc, dz, ok in ((0, -1, has_lo), (0, 1, has_hi), (-1, 0, has_prev), (1, 0, has_next)):

        @pl.when(ok)
        def _(dc=dc, dz=dz):
            pl.semaphore_signal(
                barrier, inc=1, device_id=(cut + dc, gz + dz), device_id_type=MESH
            )

    zero_halo = jnp.zeros((H,) + s1.shape[1:], jnp.float32)
    zero_c = jnp.zeros((HC,) + car.shape[1:], jnp.float32)

    @pl.when(jnp.logical_not(has_lo))
    def _():
        for ref in (s1, s2, k):
            ref[pl.ds(0, H)] = zero_halo
        for ref in (kc, car):
            ref[pl.ds(0, HC)] = zero_c

    @pl.when(jnp.logical_not(has_hi))
    def _():
        for ref in (s1, s2, k):
            ref[pl.ds(H + layers, H)] = zero_halo
        for ref in (kc, car):
            ref[pl.ds(HC + coarse, HC)] = zero_c

    load_k.wait()
    load_s.wait()
    pl.semaphore_wait(barrier, n_z + n_c)

    def remote(src, dst, index, dc, dz):
        return pltpu.make_async_remote_copy(
            src_ref=src,
            dst_ref=dst,
            send_sem=send_sem.at[index],
            recv_sem=recv_sem.at[index],
            device_id=(cut + dc, gz + dz),
            device_id_type=MESH,
        )

    class Pair:
        def __init__(self, up_src, up_dst, down_src, down_dst, index):
            self.above = remote(up_src, up_dst, index, 0, 1)
            self.below = remote(down_src, down_dst, index + 1, 0, -1)

        def each(self, when_above, act_above, when_below, act_below):
            pl.when(when_above)(act_above)
            pl.when(when_below)(act_below)

        def start(self):
            self.each(has_hi, self.above.start, has_lo, self.below.start)

        def wait_recv(self):
            self.each(has_lo, self.above.wait_recv, has_hi, self.below.wait_recv)

        def wait_send(self):
            self.each(has_hi, self.above.wait_send, has_lo, self.below.wait_send)

    k_pairs, s_pairs, b_pairs = [], [], []
    for d in range(1, H + 1):
        near, far = layers - d, d - 1
        low, high = H - d, H + layers + d - 1
        k_pairs.append(
            Pair(k.at[H + near], k.at[low], k.at[H + far], k.at[high], 4 * (d - 1))
        )
        s_pairs.append(
            Pair(s1.at[H + near], s1.at[low], s1.at[H + far], s1.at[high], 4 * (d - 1) + 2)
        )
        b_pairs.append(
            Pair(s2.at[H + near], s2.at[low], s2.at[H + far], s2.at[high], 4 * H + 2 * (d - 1))
        )
    after = 6 * H

    for d in range(H):
        k_pairs[d].start()
        s_pairs[d].start()

    fine_y = s1.shape[2]
    row = lax.broadcasted_iota(jnp.int32, (fine_y, fine_y // 2), 0)
    col = lax.broadcasted_iota(jnp.int32, (fine_y, fine_y // 2), 1)
    gather = jnp.where((row == 2 * col) | (row == 2 * col + 1), 0.125, 0.0)

    for j, value in enumerate(restricted(s1, H, coarse, tmp, gather)):
        rs[j] = value
    rs_copy = remote(rs, rs_next, after, -1, 0)
    pl.when(has_prev)(rs_copy.start)
    kc_lo, kc_hi = pl.ds(0, HC), pl.ds(HC + coarse, HC)
    kc_pair = Pair(
        kc.at[pl.ds(coarse, HC)], kc.at[kc_lo], kc.at[pl.ds(HC, HC)], kc.at[kc_hi], after + 1
    )

    lo_keep = jnp.where(has_lo, 1.0, 0.0)
    hi_keep = jnp.where(has_hi, 1.0, 0.0)

    keeps = (lo_keep, hi_keep)
    fine = Grid(H, layers, k, bx, by, bz, inv, COUPLING, keeps)
    crude = Grid(HC, coarse, kc, cx, cy, cz, cinv, 0.5 * COUPLING, keeps)
    weights = chebyshev_weights(SWEEPS)
    coarse_weights = chebyshev_weights(SWEEPS_C)

    for d in range(H + 1):
        if d > 0:
            k_pairs[d - 1].wait_recv()
        fine.coefficients(d)
        if d > 0:
            s_pairs[d - 1].wait_recv()
        fine.sweeps((s1, wa, wb, s2), weights, d)

    for pair in b_pairs:
        pair.start()

    @pl.when(has_prev)
    def _():
        for j, value in enumerate(restricted(k, H, coarse, tmp, gather)):
            kc[HC + j] = value
        kc_pair.start()

    for d in range(H + 1):
        if d > 0:
            b_pairs[d - 1].wait_recv()
        fine.sweeps((s2, wa, wb, end), weights, d)

    def send_on(dz, index, place):
        return remote(outgoing, car.at[place], index, 1, dz)

    to_same = send_on(0, after + 3, own_c)
    to_above = send_on(1, after + 4, kc_lo)
    to_below = send_on(-1, after + 5, kc_hi)

    @pl.when(has_next)
    def _():
        rs_copy.wait_recv()
        for j, value in enumerate(restricted(end, H, coarse, tmp, gather)):
            outgoing[j] = value - rs_next[j]

    @pl.when(has_prev)
    def _():
        kc_pair.wait_recv()
        for d in range(HC + 1):
            crude.coefficients(d)
        to_same.wait_recv()
        pl.when(has_lo)(to_above.wait_recv)
        pl.when(has_hi)(to_below.wait_recv)
        for d in range(HC + 1):
            crude.sweeps((car, ca, cb), coarse_weights, d)
        stepped = cb

        @pl.when(has_next)
        def _():
            outgoing[...] = outgoing[...] + stepped[own_c]

        row_s = lax.broadcasted_iota(jnp.int32, (fine_y // 2, fine_y), 0)
        col_s = lax.broadcasted_iota(jnp.int32, (fine_y // 2, fine_y), 1)
        spread = jnp.where((col_s == 2 * row_s) | (col_s == 2 * row_s + 1), 1.0, 0.0)
        rows = tmp.shape[1]
        for j in range(coarse):
            part = stepped[HC + j]
            tmp[j, pl.ds(0, rows // 2, 2), :] = part
            tmp[j, pl.ds(1, rows // 2, 2), :] = part
        wide = times_exact(jnp.concatenate([tmp[j] for j in range(coarse)], axis=0), spread)
        for l in range(layers):
            out[0, l] = end[H + l] + wide[(l // 2) * rows : (l // 2 + 1) * rows]

    @pl.when(has_next)
    def _():
        pl.when(has_hi)(to_above.start)
        pl.when(has_lo)(to_below.start)
        to_same.start()

    @pl.when(jnp.logical_not(has_prev))
    def _():
        out[0] = end[own]

    for pair in k_pairs + s_pairs + b_pairs:
        pair.wait_send()

    @pl.when(has_prev)
    def _():
        kc_pair.wait_send()
        rs_copy.wait_send()

    @pl.when(has_next)
    def _():
        to_same.wait_send()
        pl.when(has_hi)(to_above.wait_send)
        pl.when(has_lo)(to_below.wait_send)


def shards(states, conduct):
    cut_count, gz_count = lax.axis_size("cuts"), lax.axis_size("gz")
    layers, nx, ny = conduct.shape
    fine = pltpu.VMEM((layers + 2 * H, nx, ny), jnp.float32)
    coarse = pltpu.VMEM((layers // 2 + 2 * HC, nx // 2, ny // 2), jnp.float32)
    small = pltpu.VMEM((layers // 2, nx // 2, ny // 2), jnp.float32)
    return pl.pallas_call(
        functools.partial(kernel, cut_count, gz_count, layers),
        out_shape=pltpu.VMEM(states.shape, jnp.float32),
        in_specs=[pl.BlockSpec(memory_space=pl.ANY)] * 2,
        out_specs=pl.BlockSpec(memory_space=pltpu.VMEM),
        scratch_shapes=[fine] * 10
        + [pltpu.VMEM((layers // 2, nx, ny // 2), jnp.float32)]
        + [coarse] * 8
        + [small] * 3
        + [
            pltpu.SemaphoreType.DMA((2,)),
            pltpu.SemaphoreType.DMA((6 * H + 6,)),
            pltpu.SemaphoreType.DMA((6 * H + 6,)),
        ],
        compiler_params=pltpu.CompilerParams(collective_id=0, has_side_effects=True),
        name="parareal",
    )(states, conduct)


def solution(mesh):
    in_specs = (P("cuts", "gz", None, None), P("gz", None, None))
    out_specs = P("cuts", "gz", None, None)
    return jax.shard_map(shards, mesh=mesh, in_specs=in_specs, out_specs=out_specs, check_vma=False)
```

```python
import functools
import math

import jax
import jax.numpy as jnp
from jax import lax
from jax.experimental import pallas as pl
from jax.experimental.pallas import tpu as pltpu
from jax.sharding import PartitionSpec as P

STEPS = 2
SWEEPS = 3
SWEEPS_C = 2

COUPLING = 1.0
SPREAD = 0.85
H = SWEEPS
HC = SWEEPS_C
MESH = pl.DeviceIdType.MESH


def chebyshev_weights(count):
    return [
        1.0 / (1.0 + SPREAD * math.cos(math.pi * (2 * index_now + 1) / (2 * count)))
        for index_now in range(count)
    ]


def down(v, axis):
    return pltpu.roll(v, 1, axis)


def up(v, axis):
    return pltpu.roll(v, v.shape[axis] - 1, axis)


def coefficient_layer(k_ref, bx, by, inv, l, coupling, keep):
    shape = k_ref.shape[1:]
    at_x = lax.broadcasted_iota(jnp.int32, shape, 0)
    at_y = lax.broadcasted_iota(jnp.int32, shape, 1)
    half = 0.5 * coupling
    k = k_ref[l]
    x_lo = jnp.where(at_x == 0, 0.0, down(k, 0))
    x_hi = jnp.where(at_x == shape[0] - 1, 0.0, up(k, 0))
    y_lo = jnp.where(at_y == 0, 0.0, down(k, 1))
    y_hi = jnp.where(at_y == shape[1] - 1, 0.0, up(k, 1))
    bx[l] = jnp.where(at_x == 0, 0.0, half * (k + x_lo))
    by[l] = jnp.where(at_y == 0, 0.0, half * (k + y_lo))
    diag = 1.0 + half * (
        6.0 * k + (x_lo + x_hi) + (y_lo + y_hi) + (k_ref[l - 1] + k_ref[l + 1])
    )
    inv[l] = keep / diag


def sweep_layer(src, source, dst, bx, by, bz, inv, l, weight):
    w = src[l]
    b_y = by[l]
    b_x = bx[l]
    total = (
        source[l]
        + (b_y * down(w, 1) + up(b_y * w, 1))
        + (b_x * down(w, 0) + up(b_x * w, 0))
        + (bz[l] * src[l - 1] + bz[l + 1] * src[l + 1])
    )
    dst[l] = (1.0 - weight) * w + (weight * inv[l]) * total


def times_exact(value, matrix):
    high = value.astype(jnp.bfloat16)
    rest = value - high.astype(jnp.float32)
    middle = rest.astype(jnp.bfloat16)
    low = (rest - middle.astype(jnp.float32)).astype(jnp.bfloat16)
    count = value.shape[0]
    parts = lax.dot_general(
        jnp.concatenate([high, middle, low], axis=0),
        matrix.astype(jnp.bfloat16),
        (((1,), (0,)), ((), ())),
        preferred_element_type=jnp.float32,
    )
    return parts[:count] + (parts[count : 2 * count] + parts[2 * count :])


class Grid:
    def __init__(self, halo, count, k, bx, by, bz, inv, coupling, keeps):
        self.halo, self.count = halo, count
        self.k, self.bx, self.by, self.bz, self.inv = k, bx, by, bz, inv
        self.coupling = coupling
        self.keeps = keeps

    def depth(self, l):
        return max(self.halo - l, l - (self.halo + self.count - 1))

    def keep(self, l):
        return self.keeps[0] if l < self.halo else (self.keeps[1] if l >= self.halo + self.count else 1.0)

    def coefficients(self, depth):
        total = self.count + 2 * self.halo
        for l in range(1, total):
            if max(0, self.depth(l), self.depth(l - 1)) == depth:
                self.bz[l] = 0.5 * self.coupling * (self.k[l] + self.k[l - 1])
        for l in range(1, total - 1):
            if max(0, self.depth(l) + 1) == depth:
                coefficient_layer(
                    self.k, self.bx, self.by, self.inv, l, self.coupling, self.keep(l)
                )

    def sweeps(self, buffers, weights, depth):
        source = buffers[0]
        sweeps = len(weights)
        for j, weight in enumerate(weights):
            for l in range(j + 1, self.count + 2 * self.halo - 1 - j):
                if self.depth(l) > sweeps - 1 - j:
                    continue
                if max(0, self.depth(l) + j + 1) == depth:
                    sweep_layer(
                        buffers[j], source, buffers[j + 1],
                        self.bx, self.by, self.bz, self.inv, l, weight,
                    )


def restricted(field, first, pairs, tmp, matrix):
    rows = tmp.shape[1]
    sums = [field[first + 2 * j] + field[first + 2 * j + 1] for j in range(pairs)]
    narrow = times_exact(jnp.concatenate(sums, axis=0), matrix)
    half = rows // 2
    out = []
    for j in range(pairs):
        tmp[j] = narrow[j * rows : (j + 1) * rows]
        out.append(tmp[j, pl.ds(0, half, 2), :] + tmp[j, pl.ds(1, half, 2), :])
    return out


def kernel(
    cut_count, gz_count, layers,
    s_in, k_in, out,
    s1, s2, wa, wb, end, k, bx, by, bz, inv, tmp,
    kc, cx, cy, cz, cinv, car, ca, cb, rs, rs_next, outgoing,
    load_sem, send_sem, recv_sem,
):
    cut = lax.axis_index("cuts")
    gz = lax.axis_index("gz")
    has_lo, has_hi = gz > 0, gz < gz_count - 1
    has_prev, has_next = cut > 0, cut < cut_count - 1
    coarse = layers // 2
    own = pl.ds(H, layers)
    own_c = pl.ds(HC, coarse)

    load_s = pltpu.make_async_copy(s_in.at[0], s1.at[own], load_sem.at[0])
    load_k = pltpu.make_async_copy(k_in, k.at[own], load_sem.at[1])
    load_k.start()
    load_s.start()

    barrier = pltpu.get_barrier_semaphore()
    n_z = has_lo.astype(jnp.int32) + has_hi.astype(jnp.int32)
    n_c = has_prev.astype(jnp.int32) + has_next.astype(jnp.int32)
    for dc, dz, ok in ((0, -1, has_lo), (0, 1, has_hi), (-1, 0, has_prev), (1, 0, has_next)):

        @pl.when(ok)
        def _(dc=dc, dz=dz):
            pl.semaphore_signal(
                barrier, inc=1, device_id=(cut + dc, gz + dz), device_id_type=MESH
            )

    zero_halo = jnp.zeros((H,) + s1.shape[1:], jnp.float32)
    zero_c = jnp.zeros((HC,) + car.shape[1:], jnp.float32)

    @pl.when(jnp.logical_not(has_lo))
    def _():
        for ref in (s1, s2, k):
            ref[pl.ds(0, H)] = zero_halo
        for ref in (kc, car):
            ref[pl.ds(0, HC)] = zero_c

    @pl.when(jnp.logical_not(has_hi))
    def _():
        for ref in (s1, s2, k):
            ref[pl.ds(H + layers, H)] = zero_halo
        for ref in (kc, car):
            ref[pl.ds(HC + coarse, HC)] = zero_c

    load_k.wait()
    load_s.wait()
    pl.semaphore_wait(barrier, n_z + n_c)

    def remote(src, dst, index, dc, dz):
        return pltpu.make_async_remote_copy(
            src_ref=src,
            dst_ref=dst,
            send_sem=send_sem.at[index],
            recv_sem=recv_sem.at[index],
            device_id=(cut + dc, gz + dz),
            device_id_type=MESH,
        )

    class Pair:
        def __init__(self, up_src, up_dst, down_src, down_dst, index):
            self.above = remote(up_src, up_dst, index, 0, 1)
            self.below = remote(down_src, down_dst, index + 1, 0, -1)

        def each(self, when_above, act_above, when_below, act_below):
            pl.when(when_above)(act_above)
            pl.when(when_below)(act_below)

        def start(self):
            self.each(has_hi, self.above.start, has_lo, self.below.start)

        def wait_recv(self):
            self.each(has_lo, self.above.wait_recv, has_hi, self.below.wait_recv)

        def wait_send(self):
            self.each(has_hi, self.above.wait_send, has_lo, self.below.wait_send)

    k_pairs, s_pairs, b_pairs = [], [], []
    for d in range(1, H + 1):
        near, far = layers - d, d - 1
        low, high = H - d, H + layers + d - 1
        k_pairs.append(
            Pair(k.at[H + near], k.at[low], k.at[H + far], k.at[high], 4 * (d - 1))
        )
        s_pairs.append(
            Pair(s1.at[H + near], s1.at[low], s1.at[H + far], s1.at[high], 4 * (d - 1) + 2)
        )
        b_pairs.append(
            Pair(s2.at[H + near], s2.at[low], s2.at[H + far], s2.at[high], 4 * H + 2 * (d - 1))
        )
    after = 6 * H
    early_pairs = b_pairs[H - 1 :] if 2 <= H < layers else []

    for d in range(H):
        k_pairs[d].start()
        s_pairs[d].start()

    fine_y = s1.shape[2]
    row = lax.broadcasted_iota(jnp.int32, (fine_y, fine_y // 2), 0)
    col = lax.broadcasted_iota(jnp.int32, (fine_y, fine_y // 2), 1)
    gather = jnp.where((row == 2 * col) | (row == 2 * col + 1), 0.125, 0.0)

    for j, value in enumerate(restricted(s1, H, coarse, tmp, gather)):
        rs[j] = value
    rs_copy = remote(rs, rs_next, after, -1, 0)
    pl.when(has_prev)(rs_copy.start)
    kc_lo, kc_hi = pl.ds(0, HC), pl.ds(HC + coarse, HC)
    kc_pair = Pair(
        kc.at[pl.ds(coarse, HC)], kc.at[kc_lo], kc.at[pl.ds(HC, HC)], kc.at[kc_hi], after + 1
    )

    lo_keep = jnp.where(has_lo, 1.0, 0.0)
    hi_keep = jnp.where(has_hi, 1.0, 0.0)

    keeps = (lo_keep, hi_keep)
    fine = Grid(H, layers, k, bx, by, bz, inv, COUPLING, keeps)
    crude = Grid(HC, coarse, kc, cx, cy, cz, cinv, 0.5 * COUPLING, keeps)
    weights = chebyshev_weights(SWEEPS)
    coarse_weights = chebyshev_weights(SWEEPS_C)

    for d in range(H + 1):
        if d > 0:
            k_pairs[d - 1].wait_recv()
        fine.coefficients(d)
        if d > 0:
            s_pairs[d - 1].wait_recv()
        fine.sweeps((s1, wa, wb, s2), weights, d)
        if d == H - 1:
            for early in early_pairs:
                early.start()

    for pair in b_pairs:
        if pair not in early_pairs:
            pair.start()

    @pl.when(has_prev)
    def _():
        for j, value in enumerate(restricted(k, H, coarse, tmp, gather)):
            kc[HC + j] = value
        kc_pair.start()

    for d in range(H + 1):
        if d > 0:
            b_pairs[d - 1].wait_recv()
        fine.sweeps((s2, wa, wb, end), weights, d)

    def send_on(dz, index, place):
        return remote(outgoing, car.at[place], index, 1, dz)

    to_same = send_on(0, after + 3, own_c)
    to_above = send_on(1, after + 4, kc_lo)
    to_below = send_on(-1, after + 5, kc_hi)

    @pl.when(has_next)
    def _():
        rs_copy.wait_recv()
        for j, value in enumerate(restricted(end, H, coarse, tmp, gather)):
            outgoing[j] = value - rs_next[j]

    @pl.when(has_prev)
    def _():
        kc_pair.wait_recv()
        for d in range(HC + 1):
            crude.coefficients(d)
        to_same.wait_recv()
        pl.when(has_lo)(to_above.wait_recv)
        pl.when(has_hi)(to_below.wait_recv)
        for d in range(HC + 1):
            crude.sweeps((car, ca, cb), coarse_weights, d)
        stepped = cb

        @pl.when(has_next)
        def _():
            outgoing[...] = outgoing[...] + stepped[own_c]

        row_s = lax.broadcasted_iota(jnp.int32, (fine_y // 2, fine_y), 0)
        col_s = lax.broadcasted_iota(jnp.int32, (fine_y // 2, fine_y), 1)
        spread = jnp.where((col_s == 2 * row_s) | (col_s == 2 * row_s + 1), 1.0, 0.0)
        rows = tmp.shape[1]
        for j in range(coarse):
            part = stepped[HC + j]
            tmp[j, pl.ds(0, rows // 2, 2), :] = part
            tmp[j, pl.ds(1, rows // 2, 2), :] = part
        wide = times_exact(jnp.concatenate([tmp[j] for j in range(coarse)], axis=0), spread)
        for l in range(layers):
            out[0, l] = end[H + l] + wide[(l // 2) * rows : (l // 2 + 1) * rows]

    @pl.when(has_next)
    def _():
        pl.when(has_hi)(to_above.start)
        pl.when(has_lo)(to_below.start)
        to_same.start()

    @pl.when(jnp.logical_not(has_prev))
    def _():
        out[0] = end[own]

    for pair in k_pairs + s_pairs + b_pairs:
        pair.wait_send()

    @pl.when(has_prev)
    def _():
        kc_pair.wait_send()
        rs_copy.wait_send()

    @pl.when(has_next)
    def _():
        to_same.wait_send()
        pl.when(has_hi)(to_above.wait_send)
        pl.when(has_lo)(to_below.wait_send)


def shards(states, conduct):
    cut_count, gz_count = lax.axis_size("cuts"), lax.axis_size("gz")
    layers, nx, ny = conduct.shape
    fine = pltpu.VMEM((layers + 2 * H, nx, ny), jnp.float32)
    coarse = pltpu.VMEM((layers // 2 + 2 * HC, nx // 2, ny // 2), jnp.float32)
    small = pltpu.VMEM((layers // 2, nx // 2, ny // 2), jnp.float32)
    return pl.pallas_call(
        functools.partial(kernel, cut_count, gz_count, layers),
        out_shape=pltpu.VMEM(states.shape, jnp.float32),
        in_specs=[pl.BlockSpec(memory_space=pl.ANY)] * 2,
        out_specs=pl.BlockSpec(memory_space=pltpu.VMEM),
        scratch_shapes=[fine] * 10
        + [pltpu.VMEM((layers // 2, nx, ny // 2), jnp.float32)]
        + [coarse] * 8
        + [small] * 3
        + [
            pltpu.SemaphoreType.DMA((2,)),
            pltpu.SemaphoreType.DMA((6 * H + 6,)),
            pltpu.SemaphoreType.DMA((6 * H + 6,)),
        ],
        compiler_params=pltpu.CompilerParams(collective_id=0, has_side_effects=True),
        name="parareal",
    )(states, conduct)


def solution(mesh):
    in_specs = (P("cuts", "gz", None, None), P("gz", None, None))
    out_specs = P("cuts", "gz", None, None)
    return jax.shard_map(shards, mesh=mesh, in_specs=in_specs, out_specs=out_specs, check_vma=False)
```

```python
import functools
import math

import jax
import jax.numpy as jnp
from jax import lax
from jax.experimental import pallas as pl
from jax.experimental.pallas import tpu as pltpu
from jax.sharding import PartitionSpec as P

STEPS = 2
SWEEPS = 3
SWEEPS_C = 2

COUPLING = 1.0
SPREAD = 0.85
H = SWEEPS
HC = SWEEPS_C
MESH = pl.DeviceIdType.MESH


def chebyshev_weights(count):
    return [
        1.0 / (1.0 + SPREAD * math.cos(math.pi * (2 * index_now + 1) / (2 * count)))
        for index_now in range(count)
    ]


def down(v, axis):
    return pltpu.roll(v, 1, axis)


def up(v, axis):
    return pltpu.roll(v, v.shape[axis] - 1, axis)


def coefficient_layer(k_ref, bx, by, inv, l, coupling, keep):
    shape = k_ref.shape[1:]
    at_x = lax.broadcasted_iota(jnp.int32, shape, 0)
    at_y = lax.broadcasted_iota(jnp.int32, shape, 1)
    half = 0.5 * coupling
    k = k_ref[l]
    x_lo = jnp.where(at_x == 0, 0.0, down(k, 0))
    x_hi = jnp.where(at_x == shape[0] - 1, 0.0, up(k, 0))
    y_lo = jnp.where(at_y == 0, 0.0, down(k, 1))
    y_hi = jnp.where(at_y == shape[1] - 1, 0.0, up(k, 1))
    bx[l] = jnp.where(at_x == 0, 0.0, half * (k + x_lo))
    by[l] = jnp.where(at_y == 0, 0.0, half * (k + y_lo))
    diag = 1.0 + half * (
        6.0 * k + (x_lo + x_hi) + (y_lo + y_hi) + (k_ref[l - 1] + k_ref[l + 1])
    )
    inv[l] = keep / diag


def sweep_layer(src, source, dst, bx, by, bz, inv, l, weight):
    w = src[l]
    b_y = by[l]
    b_x = bx[l]
    total = (
        source[l]
        + (b_y * down(w, 1) + up(b_y * w, 1))
        + (b_x * down(w, 0) + up(b_x * w, 0))
        + (bz[l] * src[l - 1] + bz[l + 1] * src[l + 1])
    )
    dst[l] = (1.0 - weight) * w + (weight * inv[l]) * total


def times_exact(value, matrix):
    high = value.astype(jnp.bfloat16)
    rest = value - high.astype(jnp.float32)
    middle = rest.astype(jnp.bfloat16)
    low = (rest - middle.astype(jnp.float32)).astype(jnp.bfloat16)
    count = value.shape[0]
    parts = lax.dot_general(
        jnp.concatenate([high, middle, low], axis=0),
        matrix.astype(jnp.bfloat16),
        (((1,), (0,)), ((), ())),
        preferred_element_type=jnp.float32,
    )
    return parts[:count] + (parts[count : 2 * count] + parts[2 * count :])


class Grid:
    def __init__(self, halo, count, k, bx, by, bz, inv, coupling, keeps):
        self.halo, self.count = halo, count
        self.k, self.bx, self.by, self.bz, self.inv = k, bx, by, bz, inv
        self.coupling = coupling
        self.keeps = keeps

    def depth(self, l):
        return max(self.halo - l, l - (self.halo + self.count - 1))

    def keep(self, l):
        return self.keeps[0] if l < self.halo else (self.keeps[1] if l >= self.halo + self.count else 1.0)

    def coefficients(self, depth):
        total = self.count + 2 * self.halo
        for l in range(1, total):
            if max(0, self.depth(l), self.depth(l - 1)) == depth:
                self.bz[l] = 0.5 * self.coupling * (self.k[l] + self.k[l - 1])
        for l in range(1, total - 1):
            if max(0, self.depth(l) + 1) == depth:
                coefficient_layer(
                    self.k, self.bx, self.by, self.inv, l, self.coupling, self.keep(l)
                )

    def sweeps(self, buffers, weights, depth):
        source = buffers[0]
        sweeps = len(weights)
        for j, weight in enumerate(weights):
            for l in range(j + 1, self.count + 2 * self.halo - 1 - j):
                if self.depth(l) > sweeps - 1 - j:
                    continue
                if max(0, self.depth(l) + j + 1) == depth:
                    sweep_layer(
                        buffers[j], source, buffers[j + 1],
                        self.bx, self.by, self.bz, self.inv, l, weight,
                    )


def restricted(field, first, pairs, tmp, matrix):
    rows = tmp.shape[1]
    sums = [field[first + 2 * j] + field[first + 2 * j + 1] for j in range(pairs)]
    narrow = times_exact(jnp.concatenate(sums, axis=0), matrix)
    half = rows // 2
    out = []
    for j in range(pairs):
        tmp[j] = narrow[j * rows : (j + 1) * rows]
        out.append(tmp[j, pl.ds(0, half, 2), :] + tmp[j, pl.ds(1, half, 2), :])
    return out


def kernel(
    cut_count, gz_count, layers,
    s_in, k_in, out,
    s1, s2, wa, wb, end, k, bx, by, bz, inv, tmp,
    kc, cx, cy, cz, cinv, car, ca, cb, rs, rs_next, outgoing,
    load_sem, send_sem, recv_sem,
):
    cut = lax.axis_index("cuts")
    gz = lax.axis_index("gz")
    has_lo, has_hi = gz > 0, gz < gz_count - 1
    has_prev, has_next = cut > 0, cut < cut_count - 1
    coarse = layers // 2
    own = pl.ds(H, layers)
    own_c = pl.ds(HC, coarse)

    load_s = pltpu.make_async_copy(s_in.at[0], s1.at[own], load_sem.at[0])
    load_k = pltpu.make_async_copy(k_in, k.at[own], load_sem.at[1])
    load_k.start()
    load_s.start()

    barrier = pltpu.get_barrier_semaphore()
    n_z = has_lo.astype(jnp.int32) + has_hi.astype(jnp.int32)
    n_c = has_prev.astype(jnp.int32) + has_next.astype(jnp.int32)
    for dc, dz, ok in ((0, -1, has_lo), (0, 1, has_hi), (-1, 0, has_prev), (1, 0, has_next)):

        @pl.when(ok)
        def _(dc=dc, dz=dz):
            pl.semaphore_signal(
                barrier, inc=1, device_id=(cut + dc, gz + dz), device_id_type=MESH
            )

    zero_halo = jnp.zeros((H,) + s1.shape[1:], jnp.float32)
    zero_c = jnp.zeros((HC,) + car.shape[1:], jnp.float32)

    @pl.when(jnp.logical_not(has_lo))
    def _():
        for ref in (s1, s2, k):
            ref[pl.ds(0, H)] = zero_halo
        for ref in (kc, car):
            ref[pl.ds(0, HC)] = zero_c

    @pl.when(jnp.logical_not(has_hi))
    def _():
        for ref in (s1, s2, k):
            ref[pl.ds(H + layers, H)] = zero_halo
        for ref in (kc, car):
            ref[pl.ds(HC + coarse, HC)] = zero_c

    load_k.wait()
    load_s.wait()
    pl.semaphore_wait(barrier, n_z + n_c)

    def remote(src, dst, index, dc, dz):
        return pltpu.make_async_remote_copy(
            src_ref=src,
            dst_ref=dst,
            send_sem=send_sem.at[index],
            recv_sem=recv_sem.at[index],
            device_id=(cut + dc, gz + dz),
            device_id_type=MESH,
        )

    class Pair:
        def __init__(self, up_src, up_dst, down_src, down_dst, index):
            self.above = remote(up_src, up_dst, index, 0, 1)
            self.below = remote(down_src, down_dst, index + 1, 0, -1)

        def each(self, when_above, act_above, when_below, act_below):
            pl.when(when_above)(act_above)
            pl.when(when_below)(act_below)

        def start(self):
            self.each(has_hi, self.above.start, has_lo, self.below.start)

        def wait_recv(self):
            self.each(has_lo, self.above.wait_recv, has_hi, self.below.wait_recv)

        def wait_send(self):
            self.each(has_hi, self.above.wait_send, has_lo, self.below.wait_send)

    k_pairs, s_pairs, b_pairs = [], [], []
    for d in range(1, H + 1):
        near, far = layers - d, d - 1
        low, high = H - d, H + layers + d - 1
        k_pairs.append(
            Pair(k.at[H + near], k.at[low], k.at[H + far], k.at[high], 4 * (d - 1))
        )
        s_pairs.append(
            Pair(s1.at[H + near], s1.at[low], s1.at[H + far], s1.at[high], 4 * (d - 1) + 2)
        )
        b_pairs.append(
            Pair(s2.at[H + near], s2.at[low], s2.at[H + far], s2.at[high], 4 * H + 2 * (d - 1))
        )
    after = 6 * H
    early_pairs = b_pairs[H - 1 :] if 2 <= H < layers else []

    for d in range(H):
        k_pairs[d].start()
        s_pairs[d].start()

    fine_y = s1.shape[2]
    row = lax.broadcasted_iota(jnp.int32, (fine_y, fine_y // 2), 0)
    col = lax.broadcasted_iota(jnp.int32, (fine_y, fine_y // 2), 1)
    gather = jnp.where((row == 2 * col) | (row == 2 * col + 1), 0.125, 0.0)

    for j, value in enumerate(restricted(s1, H, coarse, tmp, gather)):
        rs[j] = value
    rs_copy = remote(rs, rs_next, after, -1, 0)
    pl.when(has_prev)(rs_copy.start)
    kc_lo, kc_hi = pl.ds(0, HC), pl.ds(HC + coarse, HC)
    kc_pair = Pair(
        kc.at[pl.ds(coarse, HC)], kc.at[kc_lo], kc.at[pl.ds(HC, HC)], kc.at[kc_hi], after + 1
    )

    lo_keep = jnp.where(has_lo, 1.0, 0.0)
    hi_keep = jnp.where(has_hi, 1.0, 0.0)

    keeps = (lo_keep, hi_keep)
    fine = Grid(H, layers, k, bx, by, bz, inv, COUPLING, keeps)
    crude = Grid(HC, coarse, kc, cx, cy, cz, cinv, 0.5 * COUPLING, keeps)
    weights = chebyshev_weights(SWEEPS)
    coarse_weights = chebyshev_weights(SWEEPS_C)

    for d in range(H + 1):
        if d > 0:
            k_pairs[d - 1].wait_recv()
        fine.coefficients(d)
        if d > 0:
            s_pairs[d - 1].wait_recv()
        fine.sweeps((s1, wa, wb, s2), weights, d)
        if d == H - 1:
            for early in early_pairs:
                early.start()

    for pair in b_pairs:
        if pair not in early_pairs:
            pair.start()

    @pl.when(has_prev)
    def _():
        for j, value in enumerate(restricted(k, H, coarse, tmp, gather)):
            kc[HC + j] = value
        kc_pair.start()

    for d in range(H + 1):
        if d > 0:
            b_pairs[d - 1].wait_recv()
        fine.sweeps((s2, wa, wb, end), weights, d)

    def send_on(dz, index, place):
        return remote(outgoing, car.at[place], index, 1, dz)

    to_same = send_on(0, after + 3, own_c)
    to_above = send_on(1, after + 4, kc_lo)
    to_below = send_on(-1, after + 5, kc_hi)

    @pl.when(has_next)
    def _():
        rs_copy.wait_recv()
        for j, value in enumerate(restricted(end, H, coarse, tmp, gather)):
            outgoing[j] = value - rs_next[j]

    @pl.when(has_prev)
    def _():
        kc_pair.wait_recv()
        for d in range(HC + 1):
            crude.coefficients(d)
        to_same.wait_recv()
        crude.sweeps((car, ca, cb), coarse_weights, 0)
        pl.when(has_lo)(to_above.wait_recv)
        pl.when(has_hi)(to_below.wait_recv)
        for d in range(1, HC + 1):
            crude.sweeps((car, ca, cb), coarse_weights, d)
        stepped = cb

        @pl.when(has_next)
        def _():
            outgoing[...] = outgoing[...] + stepped[own_c]

        row_s = lax.broadcasted_iota(jnp.int32, (fine_y // 2, fine_y), 0)
        col_s = lax.broadcasted_iota(jnp.int32, (fine_y // 2, fine_y), 1)
        spread = jnp.where((col_s == 2 * row_s) | (col_s == 2 * row_s + 1), 1.0, 0.0)
        rows = tmp.shape[1]
        for j in range(coarse):
            part = stepped[HC + j]
            tmp[j, pl.ds(0, rows // 2, 2), :] = part
            tmp[j, pl.ds(1, rows // 2, 2), :] = part
        wide = times_exact(jnp.concatenate([tmp[j] for j in range(coarse)], axis=0), spread)
        for l in range(layers):
            out[0, l] = end[H + l] + wide[(l // 2) * rows : (l // 2 + 1) * rows]

    @pl.when(has_next)
    def _():
        pl.when(has_hi)(to_above.start)
        pl.when(has_lo)(to_below.start)
        to_same.start()

    @pl.when(jnp.logical_not(has_prev))
    def _():
        out[0] = end[own]

    for pair in k_pairs + s_pairs + b_pairs:
        pair.wait_send()

    @pl.when(has_prev)
    def _():
        kc_pair.wait_send()
        rs_copy.wait_send()

    @pl.when(has_next)
    def _():
        to_same.wait_send()
        pl.when(has_hi)(to_above.wait_send)
        pl.when(has_lo)(to_below.wait_send)


def shards(states, conduct):
    cut_count, gz_count = lax.axis_size("cuts"), lax.axis_size("gz")
    layers, nx, ny = conduct.shape
    fine = pltpu.VMEM((layers + 2 * H, nx, ny), jnp.float32)
    coarse = pltpu.VMEM((layers // 2 + 2 * HC, nx // 2, ny // 2), jnp.float32)
    small = pltpu.VMEM((layers // 2, nx // 2, ny // 2), jnp.float32)
    return pl.pallas_call(
        functools.partial(kernel, cut_count, gz_count, layers),
        out_shape=pltpu.VMEM(states.shape, jnp.float32),
        in_specs=[pl.BlockSpec(memory_space=pl.ANY)] * 2,
        out_specs=pl.BlockSpec(memory_space=pltpu.VMEM),
        scratch_shapes=[fine] * 10
        + [pltpu.VMEM((layers // 2, nx, ny // 2), jnp.float32)]
        + [coarse] * 8
        + [small] * 3
        + [
            pltpu.SemaphoreType.DMA((2,)),
            pltpu.SemaphoreType.DMA((6 * H + 6,)),
            pltpu.SemaphoreType.DMA((6 * H + 6,)),
        ],
        compiler_params=pltpu.CompilerParams(collective_id=0, has_side_effects=True),
        name="parareal",
    )(states, conduct)


def solution(mesh):
    in_specs = (P("cuts", "gz", None, None), P("gz", None, None))
    out_specs = P("cuts", "gz", None, None)
    return jax.shard_map(shards, mesh=mesh, in_specs=in_specs, out_specs=out_specs, check_vma=False)
```
